256 devices in a mesh: lon: 32 (over z, y_hi, core), lat: 8 (over x, y_lo).
Axes of the slice: x: 4, y: 4 (y_hi: 2, y_lo: 2; y = y_hi * 2 + y_lo), z: 8, core: 2. Of those that a mesh axis runs over, the one named last changes fastest.
Arguments:
- state: bfloat16 [512, 192, 256], P(('lon', 'lat')), may hold values from -6 to 6
- cotangent: bfloat16 [512, 192, 256], P(('lon', 'lat')), may hold values from -6 to 6
- land_mask: int32 [512, 256], P(('lon', 'lat')), may hold values from 0 to 1, as said below
- neighbour_codes: int32 [512, 8], P(('lon', 'lat')), may hold values from -1 to 1023, as said below
- conv_weight: float32 [2, 49, 192], replicated, may hold values from -0.875 to 0.875
- conv_bias: float32 [2, 192], replicated, may hold values from -3 to 3
- normalizer_multiplier: float32 [2, 192], replicated, may hold values from 0.25 to 1.75
- norm_bias: float32 [2, 192], replicated, may hold values from -3 to 3
- expand_weight: bfloat16 [2, 192, 640], replicated, may hold values from -0.4375 to 0.4375
- expand_bias: float32 [2, 640], replicated, may hold values from -3 to 3
- project_weight: bfloat16 [2, 640, 192], replicated, may hold values from -0.25 to 0.25
- project_bias: float32 [2, 192], replicated, may hold values from -3 to 3
- layer_scale: float32 [2, 192], replicated, may hold values from 0.3 to 1
Outputs:
- predicted_field: bfloat16 [512, 192, 256], P(('lon', 'lat'))
- state_gradient: bfloat16 [512, 192, 256], P(('lon', 'lat'))
- conv_weight_grad: float32 [2, 49, 192], replicated
- perchannel_sensitivities: float32 [2, 5, 192], replicated
- expand_weight_grad: float32 [2, 192, 640], replicated
- expand_bias_grad: float32 [2, 640], replicated
- project_weight_grad: float32 [2, 640, 192], replicated
The draws below stay inside these ranges and needn't reach their ends.
Inputs may be any that keep to these rules, and one draw needn't show every extreme that they name: `neighbour_codes`: slots are numbered device after device, lon index slowest, 2 a device. The device at lon index a and lat index b holds in its first slots, west to east, the ocean tiles among tile columns 2 a to 2 a + 1 of tile row b; its other slots are empty and hold -1 in every direction. The code is -1 where the neighbour is land or lies south of row 0. Tile columns are cyclic. North of the top row lies the fold: tile column c beyond the top is tile column 63 - c of the top row, turned half round, and such codes carry + 512. Links are mutual. `land_mask`: every cell of an empty slot is 0.
All inputs are finite; a program needn't handle non-finite values.
Results may differ from the reference program's by a relative error of at most 0.008.
Values may be sent and summed in bfloat16 or wider, within the bound.
No kernel may reach another device: no remote copies, remote signals or barrier semaphores. Data moves between devices by JAX's collectives and lax.ppermute only.
A program may use at most 128 MiB of HBM per device.

```python
import math
import jax
import jax.numpy as jnp
from jax import lax

C = 192
HID = 640
TS = 16
SLOTS = 2
NB = 2
CELLS = 256
TILES = 512
N_LON = 32
N_LAT = 8


DIRECTIONS = ((0, 1), (0, -1), (-1, 0), (1, 0), (-1, 1), (1, 1), (-1, -1), (1, -1))


def ocean_layout(key):
    columns = SLOTS * N_LON
    draws = jax.random.randint(jax.random.fold_in(key, 5), (columns, N_LAT), 0, 10)
    block = jnp.arange(columns) // SLOTS
    forced = (block == 0) | (block == N_LON - 1)
    ocean = (draws < 7) | forced[:, None]
    wet_count = ocean.astype(jnp.int32).reshape(N_LON, SLOTS, N_LAT)
    ranking = jnp.cumsum(wet_count, axis=1) - wet_count
    matched = (wet_count[:, :, :, None] == 1) & (ranking[:, :, :, None] == jnp.arange(SLOTS)[None, None, None, :])
    living = jnp.any(matched, axis=1)
    within = jnp.sum(jnp.where(matched, jnp.arange(SLOTS)[None, :, None, None], 0), axis=1)
    column_of = within + SLOTS * jnp.arange(N_LON)[:, None, None]
    devices = jnp.arange(N_LON)[:, None, None] * N_LAT + jnp.arange(N_LAT)[None, None, :]
    tile_at = (devices * SLOTS + ranking).reshape(columns, N_LAT)
    return (ocean, living, column_of, tile_at)


def draw_neighbour_codes(key, part):
    ocean, living, column_of, tile_at = ocean_layout(key)
    columns = SLOTS * N_LON
    tile_total = columns * N_LAT
    row_of = jnp.broadcast_to(jnp.arange(N_LAT)[None, :, None], column_of.shape)
    collected = []
    for step_x, step_y in DIRECTIONS:
        target_row = row_of + step_y
        beyond = target_row > N_LAT - 1
        target_col = jnp.where(beyond, columns - 1 - (column_of + step_x), column_of + step_x) % columns
        safe_row = jnp.clip(target_row, 0, N_LAT - 1)
        found = ocean[target_col, safe_row] & (target_row >= 0) & living
        linked_code = tile_at[target_col, safe_row] + tile_total * beyond.astype(jnp.int32)
        collected.append(jnp.where(found, linked_code, -1))
    return jnp.stack(collected, axis=-1).reshape(tile_total, 8).astype(jnp.int32)


def draw_land_mask(key, part):
    ocean, living, column_of, tile_at = ocean_layout(key)
    tile_total = SLOTS * N_LON * N_LAT
    cell_draws = jax.random.randint(jax.random.fold_in(key, 11), (tile_total, TS * TS), 0, 20)
    levels = jax.random.randint(jax.random.fold_in(key, 12), (tile_total, 1), 12, 20)
    wet_cells = (cell_draws < levels) & living.reshape(tile_total, 1)
    return wet_cells.astype(jnp.int32)


def block_scale(key, dims, cuts, low, largest):
    def one(dim, blocks):
        heights = jax.random.uniform(jax.random.fold_in(jax.random.fold_in(key, 6), dim), (blocks,), jnp.float32, low / len(cuts), largest / len(cuts))
        return jnp.repeat(jnp.exp(heights), dims[dim] // blocks).reshape((-1,) + (1,) * (len(dims) - dim - 1))

    loudness = one(*cuts[0])
    for cut in cuts[1:]:
        loudness = loudness * one(*cut)
    return loudness


def scatter_about(key, shape, scale, reach, split=(), kind=jnp.bfloat16):
    entries = jax.random.normal(key, shape, jnp.float32) * scale
    if len(split) > 0:
        entries = block_scale(key, shape, split, -0.22, 0.18) * entries
    return jnp.clip(entries, min=-reach, max=reach).astype(kind)


def setup_inputs(seed: int = 0) -> dict:
    seeds = jax.random.split(jax.random.key(seed), 14)
    state = scatter_about(seeds[0], (TILES, C, CELLS), 1.0, 6.0, ((0, 256),))
    cotangent = scatter_about(seeds[1], (TILES, C, CELLS), 1.0, 6.0, ((0, 256),))
    land_mask = draw_land_mask(jax.random.fold_in(seeds[13], 71), 0)
    neighbour_codes = draw_neighbour_codes(jax.random.fold_in(seeds[13], 71), 0)
    conv_weight = scatter_about(seeds[4], (NB, 49, C), 49 ** -0.5, 0.875, (), jnp.float32)
    conv_bias = scatter_about(seeds[5], (NB, C), 0.5, 3.0, (), jnp.float32)
    normalizer_multiplier = jnp.clip(1.0 + 0.15 * jax.random.normal(seeds[6], (NB, C), jnp.float32), 0.25, 1.75)
    norm_bias = scatter_about(seeds[7], (NB, C), 0.5, 3.0, (), jnp.float32)
    expand_weight = scatter_about(seeds[8], (NB, C, HID), C ** -0.5, 0.4375)
    expand_bias = scatter_about(seeds[9], (NB, HID), 0.5, 3.0, (), jnp.float32)
    project_weight = scatter_about(seeds[10], (NB, HID, C), HID ** -0.5, 0.25)
    project_bias = scatter_about(seeds[11], (NB, C), 0.5, 3.0, (), jnp.float32)
    layer_scale = jnp.clip(jax.random.uniform(seeds[12], (NB, C), jnp.float32, 0.3, 1.0), 0.3, 1.0)
    return {"state": state, "cotangent": cotangent, "land_mask": land_mask, "neighbour_codes": neighbour_codes, "conv_weight": conv_weight, "conv_bias": conv_bias, "normalizer_multiplier": normalizer_multiplier, "norm_bias": norm_bias, "expand_weight": expand_weight, "expand_bias": expand_bias, "project_weight": project_weight, "project_bias": project_bias, "layer_scale": layer_scale}


SIDE_OPPOSITE = (1, 0, 3, 2)
CORNER_OPPOSITE = (3, 2, 1, 0)
GELU_SCALE = 0.7978845608028654
GELU_CUBIC = 0.044715

def gelu_value(values):
    inner = GELU_SCALE * (values + GELU_CUBIC * values * values * values)
    return 0.5 * values * (1.0 + jnp.tanh(inner))

def gelu_slope(values):
    tangent = jnp.tanh(GELU_SCALE * (values + GELU_CUBIC * values * values * values))
    return 0.5 * (1.0 + tangent) + 0.5 * values * (1.0 - tangent * tangent) * GELU_SCALE * (1.0 + 3.0 * GELU_CUBIC * values * values)

def cut_pieces(square, inner_low, inner_high):
    extent = square.shape[-1]
    leading = square.shape[:-2]
    side_parts = (square[..., extent - 3:, inner_low:inner_high], square[..., :3, inner_low:inner_high], square[..., inner_low:inner_high, :3], square[..., inner_low:inner_high, extent - 3:])
    corner_parts = (square[..., extent - 3:, :3], square[..., extent - 3:, extent - 3:], square[..., :3, :3], square[..., :3, extent - 3:])
    side_pieces = jnp.concatenate([section.reshape(leading + (-1,)) for section in side_parts], axis=-1)
    corner_pieces = jnp.concatenate([section.reshape(leading + (-1,)) for section in corner_parts], axis=-1)
    return (side_pieces, corner_pieces)

def linked_pieces(side_pool, corner_pool, pool_rows, flipped):
    segment = side_pool.shape[-1] // 4
    linked = []
    for which in range(4):
        fetched = side_pool[pool_rows[:, which]]
        rotated = jnp.flip(fetched[..., which * segment:(which + 1) * segment], axis=-1)
        opposite = SIDE_OPPOSITE[which]
        facing = fetched[..., opposite * segment:(opposite + 1) * segment]
        linked.append(jnp.where(flipped[:, which][:, None, None], rotated, facing))
    for which in range(4):
        fetched = corner_pool[pool_rows[:, 4 + which]]
        rotated = jnp.flip(fetched[..., which * 9:(which + 1) * 9], axis=-1)
        opposite = CORNER_OPPOSITE[which]
        facing = fetched[..., opposite * 9:(opposite + 1) * 9]
        linked.append(jnp.where(flipped[:, 4 + which][:, None, None], rotated, facing))
    return linked

def assemble(tile_grid, linked):
    tile_count, channels, extent = (tile_grid.shape[0], tile_grid.shape[1], tile_grid.shape[2])
    north_band = linked[0].reshape(tile_count, channels, 3, extent)
    south_band = linked[1].reshape(tile_count, channels, 3, extent)
    west_band = linked[2].reshape(tile_count, channels, extent, 3)
    east_band = linked[3].reshape(tile_count, channels, extent, 3)
    corners = [section.reshape(tile_count, channels, 3, 3) for section in linked[4:]]
    bottom = jnp.concatenate([corners[2], south_band, corners[3]], axis=-1)
    middle = jnp.concatenate([west_band, tile_grid, east_band], axis=-1)
    top_band = jnp.concatenate([corners[0], north_band, corners[1]], axis=-1)
    return jnp.concatenate([bottom, middle, top_band], axis=-2)

def add_border(gradient, linked):
    tile_count, channels, extent = (gradient.shape[0], gradient.shape[1], gradient.shape[2])
    side_shape = (tile_count, channels, 3, extent)
    column_shape = (tile_count, channels, extent, 3)
    corner_shape = (tile_count, channels, 3, 3)
    gradient = gradient.at[:, :, extent - 3:, :].add(linked[0].reshape(side_shape).astype(jnp.float32))
    gradient = gradient.at[:, :, :3, :].add(linked[1].reshape(side_shape).astype(jnp.float32))
    gradient = gradient.at[:, :, :, :3].add(linked[2].reshape(column_shape).astype(jnp.float32))
    gradient = gradient.at[:, :, :, extent - 3:].add(linked[3].reshape(column_shape).astype(jnp.float32))
    gradient = gradient.at[:, :, extent - 3:, :3].add(linked[4].reshape(corner_shape).astype(jnp.float32))
    gradient = gradient.at[:, :, extent - 3:, extent - 3:].add(linked[5].reshape(corner_shape).astype(jnp.float32))
    gradient = gradient.at[:, :, :3, :3].add(linked[6].reshape(corner_shape).astype(jnp.float32))
    gradient = gradient.at[:, :, :3, extent - 3:].add(linked[7].reshape(corner_shape).astype(jnp.float32))
    return gradient

def depthwise(padded, kernel, extent):
    broadened_hidden = padded.astype(jnp.float32)
    summed = jnp.zeros(padded.shape[:2] + (extent, extent), jnp.float32)
    for upward in range(7):
        for across in range(7):
            summed = summed + kernel[7 * upward + across][None, :, None, None] * broadened_hidden[:, :, upward:upward + extent, across:across + extent]
    return summed

def depthwise_adjoint(gradient, kernel, extent):
    spread = jnp.pad(gradient, ((0, 0), (0, 0), (6, 6), (6, 6)))
    summed = jnp.zeros(gradient.shape[:2] + (extent + 6, extent + 6), jnp.float32)
    for upward in range(7):
        for across in range(7):
            summed = summed + kernel[7 * upward + across][None, :, None, None] * spread[:, :, 6 - upward:12 - upward + extent, 6 - across:12 - across + extent]
    return summed

def forward_block(padded, land_part, weights):
    kernel, conv_shift, gain, norm_shift, expand_mat, expand_shift, project_mat, project_shift, scale_row = weights
    tile_count, channels, extent = (padded.shape[0], padded.shape[1], padded.shape[2] - 6)
    conv = depthwise(padded, kernel, extent) + conv_shift[None, :, None, None]
    flat = conv.reshape(tile_count, channels, extent * extent)
    average = lax.optimization_barrier(jnp.mean(flat, axis=1, keepdims=True))
    centred_values = flat - average
    inverse = lax.rsqrt(lax.optimization_barrier(jnp.mean(centred_values * centred_values, axis=1, keepdims=True)) + 1e-06)
    unit = centred_values * inverse
    normed = (unit * gain[None, :, None] + norm_shift[None, :, None]).astype(jnp.bfloat16)
    preact = jnp.einsum('ch,scp->shp', expand_mat.astype(jnp.float32), normed.astype(jnp.float32)) + expand_shift[None, :, None]
    hidden = gelu_value(preact).astype(jnp.bfloat16)
    branch = jnp.einsum('hc,shp->scp', project_mat.astype(jnp.float32), hidden.astype(jnp.float32)) + project_shift[None, :, None]
    centre_cells = padded[:, :, 3:extent + 3, 3:extent + 3].reshape(tile_count, channels, extent * extent).astype(jnp.float32)
    ocean_cells = land_part.astype(jnp.float32)[:, None, :]
    result = (ocean_cells * (centre_cells + scale_row[None, :, None] * branch)).astype(jnp.bfloat16)
    return (result, (unit, inverse, normed, preact, hidden, branch))

def backward_block(padded, land_part, weights, saved, arriving_sensitivity):
    kernel, conv_shift, gain, norm_shift, expand_mat, expand_shift, project_mat, project_shift, scale_row = weights
    unit, inverse, normed, preact, hidden, branch = saved
    tile_count, channels, extent = (padded.shape[0], padded.shape[1], padded.shape[2] - 6)
    ocean_cells = land_part.astype(jnp.float32)[:, None, :]
    masked = ocean_cells * arriving_sensitivity.astype(jnp.float32)
    branch_grad = scale_row[None, :, None] * masked
    branch_low = branch_grad.astype(jnp.bfloat16)
    hidden_grad = jnp.einsum('hc,scp->shp', project_mat.astype(jnp.float32), branch_low.astype(jnp.float32))
    preact_grad = hidden_grad * gelu_slope(preact)
    preact_low = preact_grad.astype(jnp.bfloat16)
    normed_grad = jnp.einsum('ch,shp->scp', expand_mat.astype(jnp.float32), preact_low.astype(jnp.float32))
    unit_grad = normed_grad * gain[None, :, None]
    conv_grad = inverse * (unit_grad - lax.optimization_barrier(jnp.mean(unit_grad, axis=1, keepdims=True)) - unit * lax.optimization_barrier(jnp.mean(unit_grad * unit, axis=1, keepdims=True)))
    convolution_reduced = conv_grad.astype(jnp.bfloat16)
    grad_grid = convolution_reduced.reshape(tile_count, channels, extent, extent).astype(jnp.float32)
    adjoint = depthwise_adjoint(grad_grid, kernel, extent)
    broadened_hidden = padded.astype(jnp.float32)
    kernel_grad = jnp.stack([lax.optimization_barrier(jnp.sum(grad_grid * broadened_hidden[:, :, upward:upward + extent, across:across + extent], axis=(0, 2, 3))) for upward in range(7) for across in range(7)])
    channel_grad = jnp.stack([lax.optimization_barrier(jnp.sum(conv_grad, axis=(0, 2))), lax.optimization_barrier(jnp.sum(normed_grad * unit, axis=(0, 2))), lax.optimization_barrier(jnp.sum(normed_grad, axis=(0, 2))), lax.optimization_barrier(jnp.sum(branch_grad, axis=(0, 2))), lax.optimization_barrier(jnp.sum(masked * branch, axis=(0, 2)))])
    expand_grad = jnp.einsum('scp,shp->ch', normed.astype(jnp.float32), preact_low.astype(jnp.float32))
    expand_shift_grad = lax.optimization_barrier(jnp.sum(preact_grad, axis=(0, 2)))
    project_grad = jnp.einsum('shp,scp->hc', hidden.astype(jnp.float32), branch_low.astype(jnp.float32))
    local_grad = masked.reshape(tile_count, channels, extent, extent) + adjoint[:, :, 3:extent + 3, 3:extent + 3]
    side_sent, corner_sent = cut_pieces(adjoint, 3, extent + 3)
    return (local_grad, side_sent.astype(jnp.bfloat16), corner_sent.astype(jnp.bfloat16), (kernel_grad, channel_grad, expand_grad, expand_shift_grad, project_grad))

def with_blank(pieces_all):
    return jnp.concatenate([pieces_all, jnp.zeros((1,) + pieces_all.shape[1:], pieces_all.dtype)], axis=0)

def reference(state, cotangent, land_mask, neighbour_codes, conv_weight, conv_bias, normalizer_multiplier, norm_bias, expand_weight, expand_bias, project_weight, project_bias, layer_scale):
    flipped = neighbour_codes >= TILES
    pool_rows = jnp.where(neighbour_codes < 0, TILES, neighbour_codes % TILES).astype(jnp.int32)
    batch = 4 * SLOTS
    rounds = TILES // batch
    scale_factor = 1.0 / math.sqrt(TILES * CELLS)
    masks = land_mask.reshape(rounds, batch, CELLS)

    def weights_of(layer):
        return (conv_weight[layer], conv_bias[layer], normalizer_multiplier[layer], norm_bias[layer], expand_weight[layer], expand_bias[layer], project_weight[layer], project_bias[layer], layer_scale[layer])

    def padded_of(values):
        tile_grid = values.reshape(TILES, C, TS, TS)
        side_pieces, corner_pieces = cut_pieces(tile_grid, 0, TS)
        linked = linked_pieces(with_blank(side_pieces), with_blank(corner_pieces), pool_rows, flipped)
        return assemble(tile_grid, linked)
    current_field = state
    padded_list = []
    for layer in range(NB):
        weights = weights_of(layer)
        padded = padded_of(current_field)
        padded_list.append(padded)

        def forward_round(inputs, weights=weights):
            return forward_block(inputs[0], inputs[1], weights)[0]
        current_field = lax.map(forward_round, (padded.reshape(rounds, batch, C, TS + 6, TS + 6), masks)).reshape(TILES, C, CELLS)
    predicted_field = current_field
    arriving_sensitivity = cotangent
    gradients = [None] * NB
    for layer in reversed(range(NB)):
        weights = weights_of(layer)

        def backward_round(inputs, weights=weights):
            padded_part, mask_part, upstream_part = inputs
            result, saved = forward_block(padded_part, mask_part, weights)
            return backward_block(padded_part, mask_part, weights, saved, upstream_part)
        local_grad, side_sent, corner_sent, partial_grads = lax.map(backward_round, (padded_list[layer].reshape(rounds, batch, C, TS + 6, TS + 6), masks, arriving_sensitivity.reshape(rounds, batch, C, CELLS)))
        local_grad = local_grad.reshape(TILES, C, TS, TS)
        side_sent = side_sent.reshape(TILES, C, -1)
        corner_sent = corner_sent.reshape(TILES, C, -1)
        linked = linked_pieces(with_blank(side_sent), with_blank(corner_sent), pool_rows, flipped)
        arriving_sensitivity = add_border(local_grad, linked).reshape(TILES, C, CELLS).astype(jnp.bfloat16)
        gradients[layer] = tuple((lax.optimization_barrier(jnp.sum(member, axis=0)) * scale_factor for member in partial_grads))
    batched_patches = [jnp.stack([gradients[layer][member] for layer in range(NB)]) for member in range(5)]
    return (predicted_field, arriving_sensitivity, batched_patches[0], batched_patches[1], batched_patches[2], batched_patches[3], batched_patches[4])
```

```python
import math

import jax
import jax.numpy as jnp
from jax import lax
from jax.sharding import PartitionSpec as P

GELU_SCALE = 0.7978845608028654
GELU_CUBIC = 0.044715


def gelu_value(values):
    inner = GELU_SCALE * (values + GELU_CUBIC * values * values * values)
    return 0.5 * values * (1.0 + jnp.tanh(inner))


def gelu_slope(values):
    tangent = jnp.tanh(GELU_SCALE * (values + GELU_CUBIC * values * values * values))
    return 0.5 * (1.0 + tangent) + 0.5 * values * (1.0 - tangent * tangent) * GELU_SCALE * (
        1.0 + 3.0 * GELU_CUBIC * values * values
    )


def cut_pieces(square, inner_low, inner_high):
    extent = square.shape[-1]
    leading = square.shape[:-2]
    side_parts = (
        square[..., extent - 3 :, inner_low:inner_high],
        square[..., :3, inner_low:inner_high],
        square[..., inner_low:inner_high, :3],
        square[..., inner_low:inner_high, extent - 3 :],
    )
    corner_parts = (
        square[..., extent - 3 :, :3],
        square[..., extent - 3 :, extent - 3 :],
        square[..., :3, :3],
        square[..., :3, extent - 3 :],
    )
    side_pieces = jnp.concatenate(
        [section.reshape(leading + (-1,)) for section in side_parts], axis=-1
    )
    corner_pieces = jnp.concatenate(
        [section.reshape(leading + (-1,)) for section in corner_parts], axis=-1
    )
    return (side_pieces, corner_pieces)


def assemble(tile_grid, linked):
    tile_count, channels, extent = (tile_grid.shape[0], tile_grid.shape[1], tile_grid.shape[2])
    north_band = linked[0].reshape(tile_count, channels, 3, extent)
    south_band = linked[1].reshape(tile_count, channels, 3, extent)
    west_band = linked[2].reshape(tile_count, channels, extent, 3)
    east_band = linked[3].reshape(tile_count, channels, extent, 3)
    corners = [section.reshape(tile_count, channels, 3, 3) for section in linked[4:]]
    bottom = jnp.concatenate([corners[2], south_band, corners[3]], axis=-1)
    middle = jnp.concatenate([west_band, tile_grid, east_band], axis=-1)
    top_band = jnp.concatenate([corners[0], north_band, corners[1]], axis=-1)
    return jnp.concatenate([bottom, middle, top_band], axis=-2)


def add_border(gradient, linked):
    tile_count, channels, extent = (gradient.shape[0], gradient.shape[1], gradient.shape[2])
    side_shape = (tile_count, channels, 3, extent)
    column_shape = (tile_count, channels, extent, 3)
    corner_shape = (tile_count, channels, 3, 3)
    gradient = gradient.at[:, :, extent - 3 :, :].add(
        linked[0].reshape(side_shape).astype(jnp.float32)
    )
    gradient = gradient.at[:, :, :3, :].add(linked[1].reshape(side_shape).astype(jnp.float32))
    gradient = gradient.at[:, :, :, :3].add(linked[2].reshape(column_shape).astype(jnp.float32))
    gradient = gradient.at[:, :, :, extent - 3 :].add(
        linked[3].reshape(column_shape).astype(jnp.float32)
    )
    gradient = gradient.at[:, :, extent - 3 :, :3].add(
        linked[4].reshape(corner_shape).astype(jnp.float32)
    )
    gradient = gradient.at[:, :, extent - 3 :, extent - 3 :].add(
        linked[5].reshape(corner_shape).astype(jnp.float32)
    )
    gradient = gradient.at[:, :, :3, :3].add(linked[6].reshape(corner_shape).astype(jnp.float32))
    gradient = gradient.at[:, :, :3, extent - 3 :].add(
        linked[7].reshape(corner_shape).astype(jnp.float32)
    )
    return gradient


def depthwise(padded, kernel, extent):
    broadened_hidden = padded.astype(jnp.float32)
    summed = jnp.zeros(padded.shape[:2] + (extent, extent), jnp.float32)
    for upward in range(7):
        for across in range(7):
            summed = (
                summed
                + kernel[7 * upward + across][None, :, None, None]
                * broadened_hidden[:, :, upward : upward + extent, across : across + extent]
            )
    return summed


def depthwise_adjoint(gradient, kernel, extent):
    spread = jnp.pad(gradient, ((0, 0), (0, 0), (6, 6), (6, 6)))
    summed = jnp.zeros(gradient.shape[:2] + (extent + 6, extent + 6), jnp.float32)
    for upward in range(7):
        for across in range(7):
            summed = (
                summed
                + kernel[7 * upward + across][None, :, None, None]
                * spread[:, :, 6 - upward : 12 - upward + extent, 6 - across : 12 - across + extent]
            )
    return summed


def forward_block(padded, land_part, weights):
    (
        kernel,
        conv_shift,
        gain,
        norm_shift,
        expand_mat,
        expand_shift,
        project_mat,
        project_shift,
        scale_row,
    ) = weights
    tile_count, channels, extent = (padded.shape[0], padded.shape[1], padded.shape[2] - 6)
    conv = depthwise(padded, kernel, extent) + conv_shift[None, :, None, None]
    flat = conv.reshape(tile_count, channels, extent * extent)
    average = jnp.mean(flat, axis=1, keepdims=True)
    centred_values = flat - average
    inverse = lax.rsqrt(jnp.mean(centred_values * centred_values, axis=1, keepdims=True) + 1e-06)
    unit = centred_values * inverse
    normed = (unit * gain[None, :, None] + norm_shift[None, :, None]).astype(jnp.bfloat16)
    preact = (
        jnp.einsum("ch,scp->shp", expand_mat, normed, preferred_element_type=jnp.float32)
        + expand_shift[None, :, None]
    )
    hidden = gelu_value(preact).astype(jnp.bfloat16)
    branch = (
        jnp.einsum("hc,shp->scp", project_mat, hidden, preferred_element_type=jnp.float32)
        + project_shift[None, :, None]
    )
    centre_cells = (
        padded[:, :, 3 : extent + 3, 3 : extent + 3]
        .reshape(tile_count, channels, extent * extent)
        .astype(jnp.float32)
    )
    ocean_cells = land_part.astype(jnp.float32)[:, None, :]
    result = (ocean_cells * (centre_cells + scale_row[None, :, None] * branch)).astype(jnp.bfloat16)
    return (result, (unit, inverse, normed, preact, hidden, branch))


def backward_block(padded, land_part, weights, saved, arriving_sensitivity):
    (
        kernel,
        conv_shift,
        gain,
        norm_shift,
        expand_mat,
        expand_shift,
        project_mat,
        project_shift,
        scale_row,
    ) = weights
    unit, inverse, normed, preact, hidden, branch = saved
    tile_count, channels, extent = (padded.shape[0], padded.shape[1], padded.shape[2] - 6)
    ocean_cells = land_part.astype(jnp.float32)[:, None, :]
    masked = ocean_cells * arriving_sensitivity.astype(jnp.float32)
    branch_grad = scale_row[None, :, None] * masked
    branch_low = branch_grad.astype(jnp.bfloat16)
    hidden_grad = jnp.einsum(
        "hc,scp->shp", project_mat, branch_low, preferred_element_type=jnp.float32
    )
    preact_grad = hidden_grad * gelu_slope(preact)
    preact_low = preact_grad.astype(jnp.bfloat16)
    normed_grad = jnp.einsum(
        "ch,shp->scp", expand_mat, preact_low, preferred_element_type=jnp.float32
    )
    unit_grad = normed_grad * gain[None, :, None]
    conv_grad = inverse * (
        unit_grad
        - jnp.mean(unit_grad, axis=1, keepdims=True)
        - unit * jnp.mean(unit_grad * unit, axis=1, keepdims=True)
    )
    convolution_reduced = conv_grad.astype(jnp.bfloat16)
    grad_grid = convolution_reduced.reshape(tile_count, channels, extent, extent).astype(
        jnp.float32
    )
    adjoint = depthwise_adjoint(grad_grid, kernel, extent)
    broadened_hidden = padded.astype(jnp.float32)
    kernel_grad = jnp.stack(
        [
            jnp.sum(
                grad_grid
                * broadened_hidden[:, :, upward : upward + extent, across : across + extent],
                axis=(0, 2, 3),
            )
            for upward in range(7)
            for across in range(7)
        ]
    )
    channel_grad = jnp.stack(
        [
            jnp.sum(conv_grad, axis=(0, 2)),
            jnp.sum(normed_grad * unit, axis=(0, 2)),
            jnp.sum(normed_grad, axis=(0, 2)),
            jnp.sum(branch_grad, axis=(0, 2)),
            jnp.sum(masked * branch, axis=(0, 2)),
        ]
    )
    expand_grad = jnp.einsum("scp,shp->ch", normed, preact_low, preferred_element_type=jnp.float32)
    expand_shift_grad = jnp.sum(preact_grad, axis=(0, 2))
    project_grad = jnp.einsum("shp,scp->hc", hidden, branch_low, preferred_element_type=jnp.float32)
    local_grad = (
        masked.reshape(tile_count, channels, extent, extent)
        + adjoint[:, :, 3 : extent + 3, 3 : extent + 3]
    )
    side_sent, corner_sent = cut_pieces(adjoint, 3, extent + 3)
    return (
        local_grad,
        side_sent.astype(jnp.bfloat16),
        corner_sent.astype(jnp.bfloat16),
        (kernel_grad, channel_grad, expand_grad, expand_shift_grad, project_grad),
    )


def routes(lon_count, lat_count):
    east = [(i, (i + 1) % lon_count) for i in range(lon_count)]
    west = [(i, (i - 1) % lon_count) for i in range(lon_count)]
    ahead = []
    for i in range(lon_count // 2):
        path = [i * lat_count + j for j in range(lat_count)]
        path += [(lon_count - 1 - i) * lat_count + j for j in reversed(range(lat_count))]
        ahead += list(zip(path[:-1], path[1:]))
    back = [(target, source) for source, target in ahead]
    return (east, west, ahead, back)


def link_facts(codes, slot_count):
    lon_count = lax.axis_size("lon")
    lat_count = lax.axis_size("lat")
    tile_total = slot_count * lon_count * lat_count
    lon_here = lax.axis_index("lon")
    lat_here = lax.axis_index("lat")
    turned = codes >= tile_total
    target = jnp.where(turned, codes - tile_total, codes)
    lon_there = target // (slot_count * lat_count)
    straight = jnp.where(turned, lon_count - 1 - lon_here, lon_here)
    return (
        codes >= 0,
        target % slot_count,
        lon_there == straight,
        codes[1, 2] >= 0,
        lon_here < lon_count // 2,
        lat_here == lat_count - 1,
    )


def exchange(sides, corners, facts):
    present, slot, straight, both, rising, top = facts
    side = sides.shape[-1] // 4
    corner = corners.shape[-1] // 4
    north, south, west, east = [sides[..., side * i : side * (i + 1)] for i in range(4)]
    nw, ne, sw, se = [corners[..., corner * i : corner * (i + 1)] for i in range(4)]
    join = lambda *parts: jnp.concatenate(parts, axis=-1)
    to_east, to_west, ahead, back = routes(lax.axis_size("lon"), lax.axis_size("lat"))
    eastward = join(east, ne, se)
    eastward = jnp.where(both, eastward[1], eastward[0])
    westward = join(west, nw, sw)[0]
    from_west = lax.ppermute(eastward, "lon", to_east)
    from_east = lax.ppermute(westward, "lon", to_west)
    cut = lambda message: (
        message[..., :side],
        message[..., side : side + corner],
        message[..., side + corner : side + 2 * corner],
    )
    w_side, w_ne, w_se = cut(from_west)
    e_side, e_nw, e_sw = cut(from_east)
    northward = join(north[0], north[1], nw[0], nw[1], ne[0], ne[1], w_ne, e_nw)
    southward = join(south[0], south[1], sw[0], sw[1], se[0], se[1], w_se, e_sw)
    axes = ("lon", "lat")
    got_ahead = lax.ppermute(jnp.where(rising, northward, southward), axes, ahead)
    got_back = lax.ppermute(jnp.where(rising, southward, northward), axes, back)
    from_north = jnp.where(rising, got_back, got_ahead)
    from_south = jnp.where(rising, got_ahead, got_back)

    def split(message):
        sizes = (side, side, corner, corner, corner, corner, corner, corner)
        starts = [sum(sizes[:i]) for i in range(8)]
        return [message[..., start : start + size] for start, size in zip(starts, sizes)]

    upper = split(from_north)
    turned = [jnp.flip(upper[i], axis=-1) for i in (0, 1, 4, 5, 2, 3, 7, 6)]
    upper = [jnp.where(top, turned[i], upper[i]) for i in range(8)]
    lower = split(from_south)

    def pick(which, direction):
        return lambda first, second: jnp.where(slot[which, direction] == 1, second, first)

    linked = []
    blank = lambda which, direction, piece: jnp.where(
        present[which, direction], piece, jnp.zeros_like(piece)
    )
    per_slot = []
    for which in range(2):
        pieces = [
            pick(which, 0)(upper[0], upper[1]),
            pick(which, 1)(lower[0], lower[1]),
            w_side if which == 0 else east[0],
            jnp.where(both, west[1], e_side) if which == 0 else e_side,
            jnp.where(straight[which, 4], pick(which, 4)(upper[4], upper[5]), upper[6]),
            jnp.where(straight[which, 5], pick(which, 5)(upper[2], upper[3]), upper[7]),
            jnp.where(straight[which, 6], pick(which, 6)(lower[4], lower[5]), lower[6]),
            jnp.where(straight[which, 7], pick(which, 7)(lower[2], lower[3]), lower[7]),
        ]
        per_slot.append([blank(which, e, piece) for e, piece in enumerate(pieces)])
    return [jnp.stack([per_slot[0][e], per_slot[1][e]]) for e in range(8)]


LANES = 128


def pack(gradients):
    kernel_grad, channel_grad, expand_grad, expand_shift_grad, project_grad = gradients
    layers, channels, hidden = expand_grad.shape
    rest = channels - LANES
    blocks = []
    for layer in range(layers):
        for j in range(hidden // LANES):
            blocks.append(expand_grad[layer, :, LANES * j : LANES * (j + 1)])
    for layer in range(layers):
        blocks.append(project_grad[layer, :, :LANES])
    blocks.append(jnp.concatenate([project_grad[0, :, LANES:], project_grad[1, :, LANES:]], axis=-1))
    small = jnp.concatenate([kernel_grad[0], kernel_grad[1], channel_grad[0], channel_grad[1]], axis=0)
    blocks.append(small[:, :LANES])
    blocks.append(jnp.pad(small[:, LANES:], ((0, 0), (0, LANES - rest))))
    blocks.append(expand_shift_grad.reshape(-1, LANES))
    return jnp.concatenate(blocks, axis=0)


def unpack(rows, shapes):
    (layers, taps, channels), (_, kinds, _), (_, _, hidden), _, _ = shapes
    groups = hidden // LANES
    rest = channels - LANES
    at = 0

    def take(count):
        nonlocal at
        at += count
        return rows[at - count : at]

    expand_grad = jnp.stack(
        [jnp.concatenate([take(channels) for _ in range(groups)], axis=-1) for _ in range(layers)]
    )
    heads = [take(hidden) for _ in range(layers)]
    tails = take(hidden)
    project_grad = jnp.stack(
        [
            jnp.concatenate([heads[i], tails[:, rest * i : rest * (i + 1)]], axis=-1)
            for i in range(layers)
        ]
    )
    count = layers * (taps + kinds)
    head = take(count)
    tail = take(count)
    small = jnp.concatenate([head, tail[:, :rest]], axis=-1)
    kernel_grad = small[: layers * taps].reshape(layers, taps, channels)
    channel_grad = small[layers * taps :].reshape(layers, kinds, channels)
    expand_shift_grad = take(layers * groups).reshape(layers, hidden)
    return (kernel_grad, channel_grad, expand_grad, expand_shift_grad, project_grad)


def summed(rows, scale_factor):
    lon_count = lax.axis_size("lon")
    lat_count = lax.axis_size("lat")
    quantum = 16 * lon_count * lat_count
    total = rows.shape[0]
    height = -(-total // quantum) * quantum
    low = jnp.pad(rows.astype(jnp.bfloat16), ((0, height - total), (0, 0)))

    def scattered(values, axis, count):
        parts = values.reshape(count, values.shape[0] // count, LANES)
        parts = lax.all_to_all(parts, axis, 0, 0)
        return jnp.sum(parts.astype(jnp.float32), axis=0)

    def gathered(values, axis, count):
        parts = jnp.broadcast_to(values[None], (count,) + values.shape)
        return lax.all_to_all(parts, axis, 0, 0).reshape(-1, LANES)

    mine = scattered(low, "lat", lat_count).astype(jnp.bfloat16)
    mine = (scattered(mine, "lon", lon_count) * scale_factor).astype(jnp.bfloat16)
    mine = gathered(mine, "lon", lon_count)
    return gathered(mine, "lat", lat_count)[:total].astype(jnp.float32)


def shards(
    state,
    cotangent,
    land_mask,
    neighbour_codes,
    conv_weight,
    conv_bias,
    normalizer_multiplier,
    norm_bias,
    expand_weight,
    expand_bias,
    project_weight,
    project_bias,
    layer_scale,
):
    slot_count, channels, cells = state.shape
    extent = math.isqrt(cells)
    layers = conv_weight.shape[0]
    facts = link_facts(neighbour_codes, slot_count)
    scale_factor = 1.0 / math.sqrt(slot_count * lax.axis_size("lon") * lax.axis_size("lat") * cells)

    def weights_of(layer):
        return (
            conv_weight[layer],
            conv_bias[layer],
            normalizer_multiplier[layer],
            norm_bias[layer],
            expand_weight[layer],
            expand_bias[layer],
            project_weight[layer],
            project_bias[layer],
            layer_scale[layer],
        )

    current_field = state
    padded_list = []
    saved_list = []
    for layer in range(layers):
        tile_grid = current_field.reshape(slot_count, channels, extent, extent)
        side_pieces, corner_pieces = cut_pieces(tile_grid, 0, extent)
        padded = assemble(tile_grid, exchange(side_pieces, corner_pieces, facts))
        current_field, saved = forward_block(padded, land_mask, weights_of(layer))
        padded_list.append(padded)
        saved_list.append(saved)
    arriving_sensitivity = cotangent
    gradients = [None] * layers
    for layer in reversed(range(layers)):
        local_grad, side_sent, corner_sent, partial_grads = backward_block(
            padded_list[layer],
            land_mask,
            weights_of(layer),
            saved_list[layer],
            arriving_sensitivity,
        )
        arriving_sensitivity = (
            add_border(local_grad, exchange(side_sent, corner_sent, facts))
            .reshape(slot_count, channels, cells)
            .astype(jnp.bfloat16)
        )
        gradients[layer] = partial_grads
    batched_patches = [
        jnp.stack([gradients[layer][member] for layer in range(layers)]) for member in range(5)
    ]
    shapes = [member.shape for member in batched_patches]
    totals = unpack(summed(pack(batched_patches), scale_factor), shapes)
    return (current_field, arriving_sensitivity) + totals


def solution(mesh):
    placed = (
        P(("lon", "lat"), None, None),
        P(("lon", "lat"), None, None),
        P(("lon", "lat"), None),
        P(("lon", "lat"), None),
        P(),
        P(),
        P(),
        P(),
        P(),
        P(),
        P(),
        P(),
        P(),
    )
    return jax.shard_map(
        shards,
        mesh=mesh,
        in_specs=placed,
        out_specs=(
            P(("lon", "lat"), None, None),
            P(("lon", "lat"), None, None),
            P(),
            P(),
            P(),
            P(),
            P(),
        ),
        check_vma=False,
    )
```
